32 devices in a mesh: src: 4 (over z), delay: 8 (over y, x, core).
Axes of the slice: x: 2, y: 2, z: 4, core: 2. Of those that a mesh axis runs over, the one named last changes fastest.
Arguments:
- history: float32 [32, 16, 16, 128], P('delay', 'src'), may hold values from -6 to 6
- slot_map: int32 [32], P('delay'), may hold values from 0 to 3, as said below
- interaction: float32 [1536, 128, 128], P(('src', 'delay')), may hold values from -0.0546875 to 0.0546875
- pattern: int32 [3, 1536], P(None, ('src', 'delay')), may hold values from 0 to 15, as said below
- live: int32 [32], P(('src', 'delay')), may hold values from 12 to 48
- near_inverse: float32 [16, 128, 128], P('src'), may hold values from -0.5 to 0.5
- incident: float32 [4, 16, 16, 128], P(None, 'src'), may hold values from -6 to 6
Outputs:
- currents: float32 [4, 16, 16, 128], P(None, 'src')
The draws below stay inside these ranges and needn't reach their ends.
Inputs may be any that keep to these rules, and one draw needn't show every extreme that they name: `slot_map`: each band's 4 entries are a cyclic rotation of 0 .. 3. `pattern`: row 0 lies in 0 .. 3, row 1 in 0 .. 15, row 2 in 0 .. 3.
All inputs are finite; a program needn't handle non-finite values.
Results may differ from the reference program's by a relative error of at most 0.0003.
Values sent between devices are 32-bit elements; how exact they have to be, the bound alone decides.
No kernel may reach another device: no remote copies, remote signals or barrier semaphores. Data moves between devices by JAX's collectives and lax.ppermute only.
A program may use at most 64 MiB of HBM per device.

```python
import jax
import jax.numpy as jnp
from jax import lax

BS = 128
R = 16
BLK_SRC = 4
P_DEV = 48
SLOTS = 4
STEPS = 4
NBLK = 16
PAIRS = 384
DELAYS = 32
N_SRC = 4
N_DELAY = 8


def draw_slot_map(key, part):
    offsets = jax.random.randint(key, (N_DELAY, 1), 0, SLOTS)
    within = jnp.arange(SLOTS, dtype=jnp.int32)[None, :]
    return ((within + offsets) % SLOTS).reshape(DELAYS).astype(jnp.int32)


def draw_pattern(key, part):
    total = N_SRC * PAIRS
    keys = jax.random.split(key, 3)
    rows_part = jax.random.randint(keys[0], (total,), 0, BLK_SRC)
    cols_part = jax.random.randint(keys[1], (total,), 0, NBLK)
    cols_part = cols_part.at[0].set(NBLK - 1)
    delay_part = jax.random.randint(keys[2], (total,), 0, SLOTS)
    return jnp.stack([rows_part, cols_part, delay_part]).astype(jnp.int32)


def draw_live(key, part):
    keys = jax.random.split(key, 3)
    band_index = jnp.arange(N_DELAY, dtype=jnp.int32)[None, :]
    group_index = jnp.arange(N_SRC, dtype=jnp.int32)[:, None]
    least = P_DEV // 4 + (P_DEV - P_DEV // 4) * band_index // (2 * N_DELAY)
    spread_range = P_DEV + 1 - least
    drawn = least + jax.random.randint(keys[0], (N_SRC, N_DELAY), 0, 1 << 20) % spread_range
    fullest = jax.random.randint(keys[1], (N_SRC, 1), 1, N_DELAY)
    lightest = jax.random.randint(keys[2], (), 0, N_SRC)
    drawn = jnp.where((band_index == 0) & (group_index == lightest), P_DEV // 4, drawn)
    drawn = jnp.where(band_index == fullest, P_DEV, drawn)
    return drawn.reshape(N_SRC * N_DELAY).astype(jnp.int32)


def block_scale(rng, dims, cuts, smallest, largest):
    loudness, own = 1.0, jax.random.fold_in(rng, 6)
    for axis_at, blocks in cuts:
        steps = jnp.exp(jax.random.uniform(jax.random.fold_in(own, axis_at), (blocks,), jnp.float32, smallest / len(cuts), largest / len(cuts)))
        loudness = loudness * jnp.repeat(steps, dims[axis_at] // blocks).reshape([-1 if axis == axis_at else 1 for axis in range(len(dims))])
    return loudness


def bell_draw(key, extent, spread, limit, cuts=(), kind=jnp.bfloat16):
    array = jax.random.normal(key, extent, jnp.float32) * spread
    if len(cuts) > 0:
        array = block_scale(key, extent, cuts, -0.22, 0.18) * array
    return jnp.clip(array, min=-limit, max=limit).astype(kind)


def setup_inputs(seed: int = 0) -> dict:
    streams_of = jax.random.split(jax.random.key(seed), 8)
    history = bell_draw(streams_of[0], (DELAYS, NBLK, R, BS), 1.0, 6.0, ((0, 8), (1, 4)), jnp.float32)
    slot_map = draw_slot_map(jax.random.fold_in(streams_of[7], 71), 0)
    interaction = bell_draw(streams_of[2], (N_SRC * PAIRS, BS, BS), (BS * P_DEV * N_DELAY // BLK_SRC) ** -0.5, 0.0546875, ((0, 32),), jnp.float32)
    pattern = draw_pattern(jax.random.fold_in(streams_of[7], 71), 0)
    live = draw_live(jax.random.fold_in(streams_of[7], 71), 0)
    near_inverse = bell_draw(streams_of[5], (NBLK, BS, BS), BS ** -0.5, 0.5, ((0, 4),), jnp.float32)
    incident = bell_draw(streams_of[6], (STEPS, NBLK, R, BS), 1.0, 6.0, ((1, 4),), jnp.float32)
    return {"history": history, "slot_map": slot_map, "interaction": interaction, "pattern": pattern, "live": live, "near_inverse": near_inverse, "incident": incident}


def reference(history, slot_map, interaction, pattern, live, near_inverse, incident):
    band_of = jnp.arange(DELAYS, dtype=jnp.int32) // SLOTS
    target = (band_of * SLOTS + slot_map).astype(jnp.int32)
    delayed = jnp.zeros_like(history).at[target].set(history)
    pair_rows = pattern[0].reshape(N_SRC, PAIRS)
    pair_cols = pattern[1].reshape(N_SRC, PAIRS)
    pair_band = jnp.arange(PAIRS, dtype=jnp.int32) // P_DEV
    pair_slot = jnp.arange(PAIRS, dtype=jnp.int32) % P_DEV
    pair_delay = (pair_band[None, :] * SLOTS + pattern[2].reshape(N_SRC, PAIRS)).astype(jnp.int32)
    in_use = pair_slot[None, :] < live.reshape(N_SRC, N_DELAY)[:, pair_band]
    blocks = interaction.reshape(N_SRC, PAIRS, BS, BS)
    currents = []
    for moment in range(STEPS):
        if moment > 0:
            lagged = jnp.concatenate([jnp.stack(currents[::-1]), delayed[:DELAYS - moment]], axis=0)
        else:
            lagged = delayed

        def group_field(packed):
            rows_here, cols_here, delay_here, use_here, blocks_here = packed
            picked = lagged[delay_here, cols_here]
            products = jnp.einsum("pab,prb->pra", blocks_here, picked, precision=lax.Precision.HIGHEST)
            products = jnp.where(use_here[:, None, None], products, jnp.zeros_like(products))
            onehot = (rows_here[None, :] == jnp.arange(BLK_SRC, dtype=jnp.int32)[:, None]).astype(products.dtype)
            summed = jnp.dot(onehot, products.reshape(PAIRS, R * BS), precision=lax.Precision.HIGHEST)
            return summed.reshape(BLK_SRC, R, BS)

        field_sum = lax.map(group_field, (pair_rows, pair_cols, pair_delay, in_use, blocks)).reshape(NBLK, R, BS)
        current = jnp.einsum("iab,irb->ira", near_inverse, incident[moment] - field_sum, precision=lax.Precision.HIGHEST)
        currents.append(current)
    return jnp.stack(currents)
```

```python
import functools

import jax
import jax.numpy as jnp
from jax import lax
from jax.experimental import pallas as pl
from jax.experimental.pallas import tpu as pltpu
from jax.sharding import PartitionSpec as P

F32 = jnp.float32
BF16 = jnp.bfloat16
VMEM = pltpu.VMEM
SMEM = pltpu.SMEM
UNROLL = 8


def whole(space):
    return pl.BlockSpec(memory_space=space)


def swap(x, axis, bits):
    n = lax.axis_size(axis)
    return lax.ppermute(x, axis, [(i, i ^ bits) for i in range(n)])


def halves(x):
    high = x.astype(BF16)
    low = (x - high.astype(F32)).astype(BF16)
    return high, low


def wide(x):
    high, low = halves(x)
    return jnp.concatenate([high, low], axis=-1)


def times(rows, weights):
    both = jnp.concatenate([rows, rows], axis=-1)
    return lax.dot_general(both, weights, (((1,), (1,)), ((), ())), preferred_element_type=F32)


def split_kernel(pattern, live, blocks, wide_blocks, order, counts):
    wide_blocks[...] = wide(blocks[...])
    pairs = order.shape[0]
    kinds = counts.shape[0]

    @pl.when(pl.program_id(0) == 0)
    def _():
        def place(e, at):
            kind = pattern[2, e]
            for d in range(kinds):
                @pl.when(kind == d)
                def _():
                    order[at[d]] = e
            return tuple(at[d] + (kind == d).astype(jnp.int32) for d in range(kinds))

        def count(e, n):
            kind = pattern[2, e]
            return tuple(n[d] + (kind <= d).astype(jnp.int32) for d in range(kinds))

        def clear(e, c):
            order[e] = 0
            return c

        zero = jnp.int32(0)
        lax.fori_loop(0, pairs, clear, zero)
        upto = lax.fori_loop(0, live[0], count, (zero,) * kinds)
        for d in range(kinds):
            counts[d] = upto[d]
        lax.fori_loop(0, live[0], place, (zero,) + upto[:-1])


def split_blocks(pattern, live, blocks, kinds):
    pairs, a, q = blocks.shape
    per = pairs // 6 if pairs % 6 == 0 else pairs
    return pl.pallas_call(
        split_kernel,
        grid=(pairs // per,),
        in_specs=[whole(SMEM), whole(SMEM), pl.BlockSpec((per, a, q), lambda i: (i, 0, 0))],
        out_specs=[pl.BlockSpec((per, a, 2 * q), lambda i: (i, 0, 0)), whole(SMEM), whole(SMEM)],
        out_shape=[
            jax.ShapeDtypeStruct((pairs, a, 2 * q), BF16),
            jax.ShapeDtypeStruct((pairs,), jnp.int32),
            jax.ShapeDtypeStruct((kinds,), jnp.int32),
        ],
        name="split_blocks",
    )(pattern, live, blocks)


def past_kernel(first, span, steps, me, pattern, live, slots, blocks, *refs):
    *parts, out, packed = refs
    pairs = blocks.shape[0]
    groups = len(parts)
    places, group_blocks, columns, width = parts[0].shape
    nothing = groups * places * group_blocks
    for k in range(groups):
        high, low = halves(parts[k][...].reshape(places * group_blocks, columns, width))
        packed[pl.ds(k * places * group_blocks, places * group_blocks)] = jnp.concatenate([high, low], axis=1)
    packed[nothing] = jnp.zeros((2 * columns, width), BF16)
    out[...] = jnp.zeros_like(out)
    holder = [sum(jnp.where(slots[j] == d, j, 0) for j in range(places)) for d in range(places)]

    def place_of(p):
        at = holder[0]
        for d in range(1, places):
            at = jnp.where(p == d, holder[d], at)
        return at

    def batch(i, carry):
        made = []
        for u in range(UNROLL):
            e = i * UNROLL + u
            used = e < live[0]
            e = jnp.minimum(e, pairs - 1)
            column = pattern[1, e]
            group = (column // group_blocks) ^ me[0]
            rows = []
            for t in range(steps):
                p = pattern[2, e] - first - t + span
                good = used & (p >= 0) & (p < places)
                at = (group * places + place_of(p)) * group_blocks + column % group_blocks
                rows.append(packed[jnp.where(good, at, nothing)])
            made.append((pattern[0, e], times(jnp.concatenate(rows, axis=0), blocks[e])))
        for row, y in made:
            y = y.reshape(steps, 2, columns, width)
            out[:, row] += y[:, 0] + y[:, 1]
        return carry

    lax.fori_loop(0, (live[0] + UNROLL - 1) // UNROLL, batch, 0)


def past_field(first, span, steps, me, pattern, live, slots, blocks, parts):
    places, group_blocks, columns, width = parts[0].shape
    kernel = functools.partial(past_kernel, first, span, steps)
    return pl.pallas_call(
        kernel,
        in_specs=[whole(SMEM)] * 4 + [whole(VMEM)] * (1 + len(parts)),
        out_specs=whole(VMEM),
        out_shape=jax.ShapeDtypeStruct((steps, group_blocks, columns, width), F32),
        scratch_shapes=[VMEM((len(parts) * places * group_blocks + 1, 2 * columns, width), BF16)],
        compiler_params=pltpu.CompilerParams(vmem_limit_bytes=40 << 20),
        name="past_field",
    )(me, pattern, live, slots, blocks, *parts)


def step_kernel(moment, fields, me, front, pattern, order, counts, blocks, inverse, incident, *refs):
    given = refs[:fields]
    recent = refs[fields:-3]
    out, total, packed = refs[-3:]
    group_blocks, columns, width = out.shape
    field = given[0][...]
    for f in given[1:]:
        field = field + f[...]
    total[...] = incident[moment] - field.reshape(out.shape)
    if moment:
        groups = len(recent) // moment
        nothing = moment * groups * group_blocks
        for j, ref in enumerate(recent):
            high, low = halves(ref[...])
            packed[pl.ds(j * group_blocks, group_blocks)] = jnp.concatenate([high, low], axis=1)
        packed[nothing] = jnp.zeros((2 * columns, width), BF16)
        amount = jnp.where(front[0] == 0, counts[moment - 1], 0)

        def batch(i, carry):
            made = []
            for u in range(UNROLL):
                n = i * UNROLL + u
                e = order[jnp.minimum(n, order.shape[0] - 1)]
                column = pattern[1, e]
                group = (column // group_blocks) ^ me[0]
                source = moment - 1 - pattern[2, e]
                at = (source * groups + group) * group_blocks + column % group_blocks
                made.append((pattern[0, e], times(packed[jnp.where(n < amount, at, nothing)], blocks[e])))
            for row, y in made:
                y = y.reshape(2, columns, width)
                total[row] -= y[0] + y[1]
            return carry

        lax.fori_loop(0, (amount + UNROLL - 1) // UNROLL, batch, 0)
    for i in range(group_blocks):
        high, low = halves(total[i])
        y = times(jnp.concatenate([high, low], axis=0), wide(inverse[i])).reshape(2, columns, width)
        out[i] = y[0] + y[1]


def new_currents(moment, me, front, pattern, order, counts, blocks, inverse, incident, fields, recent):
    steps, group_blocks, columns, width = incident.shape
    return pl.pallas_call(
        functools.partial(step_kernel, moment, len(fields)),
        in_specs=[whole(SMEM)] * 5 + [whole(VMEM)] * (3 + len(fields) + len(recent)),
        out_specs=whole(VMEM),
        out_shape=jax.ShapeDtypeStruct((group_blocks, columns, width), F32),
        scratch_shapes=[
            VMEM((group_blocks, columns, width), F32),
            VMEM((len(recent) * group_blocks + 1, 2 * columns, width), BF16),
        ],
        compiler_params=pltpu.CompilerParams(vmem_limit_bytes=40 << 20),
        name="new_currents",
    )(me, front, pattern, order, counts, blocks, inverse, incident, *fields, *recent)


def summands(x):
    bands = lax.axis_size("delay")
    x = x + swap(x, "delay", 1)
    if bands <= 8:
        return [x] + [swap(x, "delay", k) for k in range(2, bands, 2)]
    bit = 2
    while bit < bands:
        x = x + swap(x, "delay", bit)
        bit *= 2
    return [x]


def from_front(x):
    bands = lax.axis_size("delay")
    mine = lax.axis_index("delay")
    bit = bands // 2
    while bit:
        other = swap(x, "delay", bit)
        x = jnp.where((mine & bit) != 0, other, x)
        bit //= 2
    return x


def body(history, slot_map, interaction, pattern, live, near_inverse, incident):
    slot_count = history.shape[0]
    moments = incident.shape[0]
    groups = lax.axis_size("src")
    bands = lax.axis_size("delay")
    assert moments - 1 <= slot_count
    assert groups & (groups - 1) == 0 and bands & (bands - 1) == 0
    me = lax.axis_index("src").reshape(1)
    front = lax.axis_index("delay").reshape(1)

    parts = [history] + [swap(history, "src", k) for k in range(1, groups)]
    blocks, order, counts = split_blocks(pattern, live, interaction, slot_count)
    field = past_field(0, 0, moments, me, pattern, live, slot_map, blocks, parts)

    late = moments - 1
    ring = [(i, (i + 1) % bands) for i in range(bands)]
    slots_before = lax.ppermute(slot_map, "delay", ring)
    before = [lax.ppermute(p, "delay", ring) for p in parts]
    live_before = jnp.where(front == 0, 0, live)
    more = past_field(1, slot_count, late, me, pattern, live_before, slots_before, blocks, before)

    first_fields = summands(field[0])
    later_fields = summands(field[1:] + more)
    step = functools.partial(new_currents, me=me, front=front, pattern=pattern, order=order, counts=counts,
                             blocks=blocks, inverse=near_inverse, incident=incident)
    results = [step(0, fields=first_fields, recent=[])]
    recent = []
    for moment in range(1, moments):
        newest = results[-1]
        recent = recent + [newest] + [swap(newest, "src", k) for k in range(1, groups)]
        results.append(step(moment, fields=[f[moment - 1] for f in later_fields], recent=recent))
    return jnp.concatenate([results[0][None], from_front(jnp.stack(results[1:]))])


def solution(mesh):
    return jax.shard_map(
        body,
        mesh=mesh,
        in_specs=(
            P("delay", "src", None, None),
            P("delay"),
            P(("src", "delay"), None, None),
            P(None, ("src", "delay")),
            P(("src", "delay")),
            P("src", None, None),
            P(None, "src", None, None),
        ),
        out_specs=P(None, "src", None, None),
        check_vma=False,
    )
```

```python
import functools

import jax
import jax.numpy as jnp
from jax import lax
from jax.experimental import pallas as pl
from jax.experimental.pallas import tpu as pltpu
from jax.sharding import PartitionSpec as P

F32 = jnp.float32
BF16 = jnp.bfloat16
VMEM = pltpu.VMEM
SMEM = pltpu.SMEM
UNROLL = 16


def whole(space):
    return pl.BlockSpec(memory_space=space)


def swap(x, axis, bits):
    n = lax.axis_size(axis)
    return lax.ppermute(x, axis, [(i, i ^ bits) for i in range(n)])


def halves(x):
    high = x.astype(BF16)
    low = (x - high.astype(F32)).astype(BF16)
    return high, low


def wide(x):
    high, low = halves(x)
    return jnp.concatenate([high, low], axis=-1)


def times(rows, weights):
    both = jnp.concatenate([rows, rows], axis=-1)
    return lax.dot_general(both, weights, (((1,), (1,)), ((), ())), preferred_element_type=F32)


def room(pairs):
    return (pairs + UNROLL - 1) // UNROLL * UNROLL + UNROLL


def plan_kernel(groups, group_blocks, steps, me, band, pattern, live, slots, past, newer, held, count):
    places = slots.shape[0]
    size = room(pattern.shape[1])
    cells = places * group_blocks
    for d in range(places):
        held[d] = sum(jnp.where(slots[j] == d, j, 0) for j in range(places))
        count[d] = 0
    wide_entry, late_entry, late_start = 2 + steps, 1 + steps, 3 + 2 * size * (2 + steps)

    def place(e, near):
        row, column, d = pattern[0, e], pattern[1, e], pattern[2, e]
        group = (column // group_blocks) ^ me[0]
        block = column % group_blocks
        is_far = (group >= 2).astype(jnp.int32)
        to = 3 + (is_far * size + jnp.where(is_far == 1, e - near, near)) * wide_entry
        past[to] = e
        past[to + 1] = row
        for t in range(steps):
            at = ((group - 2 * is_far) * places + held[jnp.maximum(d - t, 0)]) * group_blocks + block
            nothing = jnp.where(is_far == 1, (groups - 2) * cells, 2 * cells)
            past[to + 2 + t] = jnp.where(d >= t, at, nothing)
        to = late_start + e * late_entry
        past[to] = e
        past[to + 1] = row
        for t in range(1, steps):
            at = (group * places + d - t + places) * group_blocks + block
            past[to + 1 + t] = jnp.where(d < t, at, groups * cells)
        n = count[d]
        count[d] = n + 1
        to = places + (d * size + n) * 3
        newer[to] = e
        newer[to + 1] = row
        newer[to + 2] = group * group_blocks + block
        return near + 1 - is_far

    near = lax.fori_loop(0, live[0], place, jnp.int32(0))
    far = live[0] - near
    past[0] = near
    past[1] = far
    past[2] = jnp.where(band[0] == 0, 0, live[0])

    def fill(i, c):
        for k, n, nothing in ((0, near, 2 * cells), (1, far, (groups - 2) * cells)):
            to = 3 + (k * size + n + i) * wide_entry
            past[to] = 0
            past[to + 1] = 0
            for t in range(steps):
                past[to + 2 + t] = nothing
        to = late_start + (live[0] + i) * late_entry
        past[to] = 0
        past[to + 1] = 0
        for t in range(1, steps):
            past[to + 1 + t] = groups * cells
        for d in range(places):
            to = places + (d * size + count[d] + i) * 3
            newer[to] = 0
            newer[to + 1] = 0
            newer[to + 2] = groups * group_blocks
        return c

    lax.fori_loop(0, UNROLL, fill, 0)
    for d in range(places):
        newer[d] = jnp.where(band[0] == 0, count[d], 0)


def make_plan(groups, group_blocks, steps, me, band, pattern, live, slots):
    places = slots.shape[0]
    size = room(pattern.shape[1])
    return pl.pallas_call(
        functools.partial(plan_kernel, groups, group_blocks, steps),
        in_specs=[whole(SMEM)] * 5,
        out_specs=[whole(SMEM)] * 2,
        out_shape=[
            jax.ShapeDtypeStruct((3 + size * (2 * (2 + steps) + 1 + steps),), jnp.int32),
            jax.ShapeDtypeStruct((places + places * size * 3,), jnp.int32),
        ],
        scratch_shapes=[SMEM((places,), jnp.int32), SMEM((places,), jnp.int32)],
        name="make_plan",
    )(me, band, pattern, live, slots)


def split_kernel(blocks, inverse, wide_blocks, wide_inverse, held, held_inverse, sems):
    chunks = sems.shape[0] - 1
    per = blocks.shape[0] // chunks
    copies = [
        pltpu.make_async_copy(blocks.at[pl.ds(k * per, per)], held.at[pl.ds(k * per, per)], sems.at[k])
        for k in range(chunks)
    ]
    copies.append(pltpu.make_async_copy(inverse, held_inverse, sems.at[chunks]))
    for c in copies:
        c.start()
    for k in range(chunks):
        copies[k].wait()

        def split(e, c):
            wide_blocks[e] = wide(held[e])
            return c

        lax.fori_loop(k * per, (k + 1) * per, split, 0, unroll=4)
    copies[chunks].wait()
    wide_inverse[...] = wide(held_inverse[...])


def split_blocks(blocks, inverse):
    pairs, a, q = blocks.shape
    chunks = 4 if pairs % 4 == 0 else 1
    return pl.pallas_call(
        split_kernel,
        in_specs=[whole(pltpu.HBM)] * 2,
        out_specs=[whole(VMEM)] * 2,
        out_shape=[
            jax.ShapeDtypeStruct((pairs, a, 2 * q), BF16),
            jax.ShapeDtypeStruct((inverse.shape[0], a, 2 * q), BF16),
        ],
        scratch_shapes=[VMEM(blocks.shape, F32), VMEM(inverse.shape, F32), pltpu.SemaphoreType.DMA((chunks + 1,))],
        compiler_params=pltpu.CompilerParams(vmem_limit_bytes=16 << 20),
        cost_estimate=pl.CostEstimate(flops=8 * pairs * a * q, bytes_accessed=8 * pairs * a * q, transcendentals=0),
        name="split_blocks",
    )(blocks, inverse)


def pack(packed, start, x):
    high, low = halves(x)
    packed[pl.ds(start, x.shape[0])] = jnp.concatenate([high, low], axis=1)


def batches(plan, start, entry, amount, packed, blocks, add):
    def batch(i, carry):
        made = []
        for u in range(UNROLL):
            at = start + (i * UNROLL + u) * entry
            rows = [packed[plan[at + 2 + t]] for t in range(entry - 2)]
            made.append((plan[at + 1], times(jnp.concatenate(rows, axis=0), blocks[plan[at]])))
        for row, y in made:
            y = y.reshape(entry - 2, 2, packed.shape[1] // 2, y.shape[-1])
            add(row, y[:, 0] + y[:, 1])
        return carry

    lax.fori_loop(0, (amount + UNROLL - 1) // UNROLL, batch, 0)


def past_kernel(when, plan, *refs):
    if when == "near":
        blocks, *parts, out, packed = refs
        out[...] = jnp.zeros_like(out)
    elif when == "far":
        blocks, base, *parts, out, now, packed = refs
        out[...] = base[...]
    else:
        slots, blocks, base, *parts, out, packed = refs
        out[...] = base[1:]
    places, group_blocks, columns, width = parts[0].shape
    cells = places * group_blocks
    for k in range(len(parts)):
        if when == "late":
            for j in range(places):
                pack(packed, (k * places + slots[j]) * group_blocks, parts[k][j])
        else:
            pack(packed, k * cells, parts[k][...].reshape(cells, columns, width))
    packed[len(parts) * cells] = jnp.zeros((2 * columns, width), BF16)
    size = room(blocks.shape[0])
    which = ("near", "far", "late").index(when)
    entry = 2 + out.shape[0]
    start = 3 + which * size * (entry + which // 2)

    def add(row, y):
        out[:, row] += y

    batches(plan, start, entry, plan[which], packed, blocks, add)
    if when == "far":
        now[...] = out[0]


def past_field(when, steps, plan, blocks, parts, base=None, slots=None):
    places, group_blocks, columns, width = parts[0].shape
    shape = (group_blocks, columns, width)
    packed = VMEM((len(parts) * places * group_blocks + 1, 2 * columns, width), BF16)
    out = [jax.ShapeDtypeStruct((steps - (when == "late"),) + shape, F32)]
    if when == "far":
        out.append(jax.ShapeDtypeStruct(shape, F32))
    scalars = [plan] + [slots] * (when == "late")
    given = [blocks] + [base] * (when != "near")
    return pl.pallas_call(
        functools.partial(past_kernel, when),
        in_specs=[whole(SMEM)] * len(scalars) + [whole(VMEM)] * (len(given) + len(parts)),
        out_specs=[whole(VMEM)] * len(out),
        out_shape=out,
        scratch_shapes=[packed],
        compiler_params=pltpu.CompilerParams(vmem_limit_bytes=16 << 20),
        name=when + "_field",
    )(*scalars, *given, *parts)


def solve(inverse, right, out):
    for i in range(out.shape[0]):
        high, low = halves(right[i])
        y = times(jnp.concatenate([high, low], axis=0), inverse[i]).reshape((2,) + out.shape[1:])
        out[i] = y[0] + y[1]


def summed(refs, t):
    total = refs[0][t]
    for r in refs[1:]:
        total = total + r[t]
    return total


def first_kernel(inverse, incident, *refs):
    *terms, out, right = refs
    right[...] = incident[0] - summed(terms, ...)
    solve(inverse, right, out)


def first_currents(inverse, incident, terms):
    shape = incident.shape[1:]
    return pl.pallas_call(
        first_kernel,
        in_specs=[whole(VMEM)] * (2 + len(terms)),
        out_specs=whole(VMEM),
        out_shape=jax.ShapeDtypeStruct(shape, F32),
        scratch_shapes=[VMEM(shape, F32)],
        compiler_params=pltpu.CompilerParams(vmem_limit_bytes=16 << 20),
        name="first_currents",
    )(inverse, incident, *terms)


def recent(kind, plan, places, packed, blocks, add):
    start = places + kind * room(blocks.shape[0]) * 3
    batches(plan, start, 3, plan[kind], packed, blocks, lambda row, y: add(row, y[0]))


def right_side(rights, t):
    if len(rights) == 1:
        return rights[0][t]
    return rights[0][t + 1] - summed(rights[1:], t)


def step_kernel(places, count, plan, blocks, inverse, *refs):
    rights, parts, (out, packed, right) = refs[:count], refs[count:-3], refs[-3:]
    group_blocks, columns, width = out.shape
    for k in range(len(parts)):
        pack(packed, k * group_blocks, parts[k][...])
    packed[len(parts) * group_blocks] = jnp.zeros((2 * columns, width), BF16)
    right[...] = right_side(rights, 0)

    def add(row, y):
        right[row] -= y

    recent(0, plan, places, packed, blocks, add)
    solve(inverse, right, out)


def next_currents(places, plan, blocks, inverse, rights, parts):
    shape = parts[0].shape
    packed = (len(parts) * shape[0] + 1, 2 * shape[1], shape[2])
    return pl.pallas_call(
        functools.partial(step_kernel, places, len(rights)),
        in_specs=[whole(SMEM)] + [whole(VMEM)] * (2 + len(rights) + len(parts)),
        out_specs=[whole(VMEM)] * 2,
        out_shape=[jax.ShapeDtypeStruct(shape, F32), jax.ShapeDtypeStruct(packed, BF16)],
        scratch_shapes=[VMEM(shape, F32)],
        compiler_params=pltpu.CompilerParams(vmem_limit_bytes=16 << 20),
        name="next_currents",
    )(plan, blocks, inverse, *rights, *parts)


def older_kernel(places, plan, blocks, packed, newest, *refs):
    *rights, out, passed = refs
    passed[...] = newest[...]
    for t in range(out.shape[0]):
        out[t] = right_side(rights, t + 1)

        def add(row, y):
            out[t, row] -= y

        recent(t + 1, plan, places, packed, blocks, add)


def older_field(places, steps, plan, blocks, packed, newest, rights):
    return pl.pallas_call(
        functools.partial(older_kernel, places),
        in_specs=[whole(SMEM)] + [whole(VMEM)] * (3 + len(rights)),
        out_specs=[whole(VMEM)] * 2,
        out_shape=[jax.ShapeDtypeStruct((steps,) + newest.shape, F32), jax.ShapeDtypeStruct(newest.shape, F32)],
        compiler_params=pltpu.CompilerParams(vmem_limit_bytes=16 << 20),
        name="older_field",
    )(plan, blocks, packed, newest, *rights)


def summands(x):
    bands = lax.axis_size("delay")
    if bands <= 8:
        return [x] + [swap(x, "delay", k) for k in range(2, bands, 2)]
    return [doubled(x)]


def front_summands(x):
    bands = lax.axis_size("delay")
    if bands > 8:
        return [doubled(x)]
    terms = [x]
    for c in range(bands - 2, 0, -2):
        goes = {i: i ^ 1 for i in range(bands)} | {c: 0, 0: 1, 1: c + 1, c + 1: c}
        terms.append(lax.ppermute(x, "delay", list(goes.items())))
    return terms


def doubled(x):
    bit = 2
    while bit < lax.axis_size("delay"):
        x = x + swap(x, "delay", bit)
        bit *= 2
    return x


def from_front(x):
    bands = lax.axis_size("delay")
    mine = lax.axis_index("delay")
    bit = bands // 2
    while bit > 1:
        goes = {i: i ^ 1 for i in range(bands)}
        for i in range(0, bands, 2 * bit):
            goes |= {i: i + bit, i + bit: i + bit + 1, i + bit + 1: i + 1, i + 1: i}
        other = lax.ppermute(x, "delay", list(goes.items()))
        x = jnp.where((mine & (2 * bit - 1)) == bit, other, x)
        bit //= 2
    return x


def from_even(x):
    return jnp.where((lax.axis_index("delay") & 1) != 0, swap(x, "delay", 1), x)


def body(history, slot_map, interaction, pattern, live, near_inverse, incident):
    slot_count = history.shape[0]
    moments = incident.shape[0]
    groups = lax.axis_size("src")
    bands = lax.axis_size("delay")
    assert moments - 1 <= slot_count and moments % 2 == 0
    assert groups & (groups - 1) == 0 and bands & (bands - 1) == 0
    me = lax.axis_index("src").reshape(1)
    band = lax.axis_index("delay").reshape(1)

    def front_over_src(x):
        pairs = [[(i * bands + j, (i ^ k) * bands if j == 0 else i * bands + j % (bands - 1) + 1)
                  for i in range(groups) for j in range(bands)] for k in range(1, groups)]
        return [x] + [lax.ppermute(x, ("src", "delay"), p) for p in pairs]

    parts = [history] + [swap(history, "src", k) for k in range(1, groups)]
    ring = [(i, (i + 1) % bands) for i in range(bands)]
    slots_before = lax.ppermute(slot_map, "delay", ring)
    blocks, inverse = split_blocks(interaction, near_inverse)
    past, newer = make_plan(groups, history.shape[1], moments, me, band, pattern, live, slot_map)
    parts[1], slots_before, past, newer, blocks, inverse = lax.optimization_barrier(
        (parts[1], slots_before, past, newer, blocks, inverse)
    )
    (field,) = past_field("near", moments, past, blocks, parts[:2])
    field, parts[2:] = lax.optimization_barrier((field, parts[2:]))
    before = [lax.ppermute(p, "delay", ring) for p in parts]
    field, now = past_field("far", moments, past, blocks, parts[2:], field)
    now = now + swap(now, "delay", 1)
    now, field = lax.optimization_barrier((now, field))
    (later,) = past_field("late", moments, past, blocks, before, field, slots_before)

    newest = first_currents(inverse, incident, summands(now))
    results = [newest]
    rights = None
    for moment in range(1, moments):
        shared = front_over_src(newest)
        if moment == 1:
            rights = [incident] + front_summands(later + swap(later, "delay", 1))
        else:
            rights, newest = older_field(slot_count, moments - moment, newer, blocks, packed, newest, rights)
            rights = [rights]
            results.append(from_even(from_front(newest)))
        newest, packed = next_currents(slot_count, newer, blocks, inverse, rights, shared)
    results.append(from_even(from_front(newest)))
    return jnp.stack(results)


def solution(mesh):
    return jax.shard_map(
        body,
        mesh=mesh,
        in_specs=(
            P("delay", "src", None, None),
            P("delay"),
            P(("src", "delay"), None, None),
            P(None, ("src", "delay")),
            P(("src", "delay")),
            P("src", None, None),
            P(None, "src", None, None),
        ),
        out_specs=P(None, "src", None, None),
        check_vma=False,
    )
```

```python
import functools

import jax
import jax.numpy as jnp
from jax import lax
from jax.experimental import pallas as pl
from jax.experimental.pallas import tpu as pltpu
from jax.sharding import PartitionSpec as P

F32 = jnp.float32
BF16 = jnp.bfloat16
VMEM = pltpu.VMEM
SMEM = pltpu.SMEM
UNROLL = 16
BRIEF = pl.CostEstimate(flops=1, bytes_accessed=1, transcendentals=0)


def whole(space):
    return pl.BlockSpec(memory_space=space)


def swap(x, axis, bits):
    n = lax.axis_size(axis)
    return lax.ppermute(x, axis, [(i, i ^ bits) for i in range(n)])


def halves(x):
    high = x.astype(BF16)
    low = (x - high.astype(F32)).astype(BF16)
    return high, low


def wide(x):
    high, low = halves(x)
    return jnp.concatenate([high, low], axis=-1)


def times(rows, weights):
    both = jnp.concatenate([rows, rows], axis=-1)
    return lax.dot_general(both, weights, (((1,), (1,)), ((), ())), preferred_element_type=F32)


def room(pairs):
    return (pairs + UNROLL - 1) // UNROLL * UNROLL + UNROLL


def plan_kernel(groups, group_blocks, steps, me, band, pattern, live, slots, past, newer, held, count):
    places = slots.shape[0]
    size = room(pattern.shape[1])
    cells = places * group_blocks
    for d in range(places):
        held[d] = sum(jnp.where(slots[j] == d, j, 0) for j in range(places))
        count[d] = 0
    wide_entry, late_entry, late_start = 2 + steps, 1 + steps, 3 + 2 * size * (2 + steps)

    def place(e, taken):
        near, few = taken
        row, column, d = pattern[0, e], pattern[1, e], pattern[2, e]
        group = (column // group_blocks) ^ me[0]
        block = column % group_blocks
        is_far = (group >= 2).astype(jnp.int32)
        to = 3 + (is_far * size + jnp.where(is_far == 1, e - near, near)) * wide_entry
        past[to] = e
        past[to + 1] = row
        for t in range(steps):
            at = ((group - 2 * is_far) * places + held[jnp.maximum(d - t, 0)]) * group_blocks + block
            nothing = jnp.where(is_far == 1, (groups - 2) * cells, 2 * cells)
            past[to + 2 + t] = jnp.where(d >= t, at, nothing)
        to = late_start + few * late_entry
        past[to] = e
        past[to + 1] = row
        for t in range(1, steps):
            at = (group * places + d - t + places) * group_blocks + block
            past[to + 1 + t] = jnp.where(d < t, at, groups * cells)
        n = count[d]
        count[d] = n + 1
        to = places + (d * size + n) * 3
        newer[to] = e
        newer[to + 1] = row
        newer[to + 2] = group * group_blocks + block
        return near + 1 - is_far, few + (d < steps - 1).astype(jnp.int32)

    near, few = lax.fori_loop(0, live[0], place, (jnp.int32(0), jnp.int32(0)))
    far = live[0] - near
    past[0] = near
    past[1] = far
    past[2] = jnp.where(band[0] == 0, 0, few)

    def fill(i, c):
        for k, n, nothing in ((0, near, 2 * cells), (1, far, (groups - 2) * cells)):
            to = 3 + (k * size + n + i) * wide_entry
            past[to] = 0
            past[to + 1] = 0
            for t in range(steps):
                past[to + 2 + t] = nothing
        to = late_start + (few + i) * late_entry
        past[to] = 0
        past[to + 1] = 0
        for t in range(1, steps):
            past[to + 1 + t] = groups * cells
        for d in range(places):
            to = places + (d * size + count[d] + i) * 3
            newer[to] = 0
            newer[to + 1] = 0
            newer[to + 2] = groups * group_blocks
        return c

    lax.fori_loop(0, UNROLL, fill, 0)
    for d in range(places):
        newer[d] = jnp.where(band[0] == 0, count[d], 0)


def make_plan(groups, group_blocks, steps, me, band, pattern, live, slots):
    places = slots.shape[0]
    size = room(pattern.shape[1])
    return pl.pallas_call(
        functools.partial(plan_kernel, groups, group_blocks, steps),
        in_specs=[whole(SMEM)] * 5,
        out_specs=[whole(SMEM)] * 2,
        out_shape=[
            jax.ShapeDtypeStruct((3 + size * (2 * (2 + steps) + 1 + steps),), jnp.int32),
            jax.ShapeDtypeStruct((places + places * size * 3,), jnp.int32),
        ],
        scratch_shapes=[SMEM((places,), jnp.int32), SMEM((places,), jnp.int32)],
        name="make_plan",
    )(me, band, pattern, live, slots)


def split_kernel(blocks, inverse, wide_blocks, wide_inverse, held, held_inverse, sems):
    chunks = sems.shape[0] - 1
    per = blocks.shape[0] // chunks
    copies = [
        pltpu.make_async_copy(blocks.at[pl.ds(k * per, per)], held.at[pl.ds(k * per, per)], sems.at[k])
        for k in range(chunks)
    ]
    copies.append(pltpu.make_async_copy(inverse, held_inverse, sems.at[chunks]))
    for c in copies:
        c.start()
    for k in range(chunks):
        copies[k].wait()

        def split(e, c):
            wide_blocks[e] = wide(held[e])
            return c

        lax.fori_loop(k * per, (k + 1) * per, split, 0, unroll=4)
    copies[chunks].wait()
    wide_inverse[...] = wide(held_inverse[...])


def split_blocks(blocks, inverse):
    pairs, a, q = blocks.shape
    chunks = 4 if pairs % 4 == 0 else 1
    return pl.pallas_call(
        split_kernel,
        in_specs=[whole(pltpu.HBM)] * 2,
        out_specs=[whole(VMEM)] * 2,
        out_shape=[
            jax.ShapeDtypeStruct((pairs, a, 2 * q), BF16),
            jax.ShapeDtypeStruct((inverse.shape[0], a, 2 * q), BF16),
        ],
        scratch_shapes=[VMEM(blocks.shape, F32), VMEM(inverse.shape, F32), pltpu.SemaphoreType.DMA((chunks + 1,))],
        compiler_params=pltpu.CompilerParams(vmem_limit_bytes=16 << 20),
        cost_estimate=pl.CostEstimate(flops=8 * pairs * a * q, bytes_accessed=8 * pairs * a * q, transcendentals=0),
        name="split_blocks",
    )(blocks, inverse)


def pack(packed, start, x):
    high, low = halves(x)
    packed[pl.ds(start, x.shape[0])] = jnp.concatenate([high, low], axis=1)


def batches(plan, start, entry, amount, packed, blocks, add):
    def batch(i, carry):
        made = []
        for u in range(UNROLL):
            at = start + (i * UNROLL + u) * entry
            rows = [packed[plan[at + 2 + t]] for t in range(entry - 2)]
            made.append((plan[at + 1], times(jnp.concatenate(rows, axis=0), blocks[plan[at]])))
        for row, y in made:
            y = y.reshape(entry - 2, 2, packed.shape[1] // 2, y.shape[-1])
            add(row, y[:, 0] + y[:, 1])
        return carry

    lax.fori_loop(0, (amount + UNROLL - 1) // UNROLL, batch, 0)


def past_kernel(when, plan, *refs):
    if when == "near":
        blocks, *parts, out, packed = refs
        out[...] = jnp.zeros_like(out)
    elif when == "far":
        blocks, base, *parts, out, now, packed = refs
        out[...] = base[...]
    else:
        slots, blocks, base, *parts, out, packed = refs
        out[...] = base[1:]
    places, group_blocks, columns, width = parts[0].shape
    cells = places * group_blocks
    for k in range(len(parts)):
        if when == "late":
            for j in range(places):
                pack(packed, (k * places + slots[j]) * group_blocks, parts[k][j])
        else:
            pack(packed, k * cells, parts[k][...].reshape(cells, columns, width))
    packed[len(parts) * cells] = jnp.zeros((2 * columns, width), BF16)
    size = room(blocks.shape[0])
    which = ("near", "far", "late").index(when)
    entry = 2 + out.shape[0]
    start = 3 + which * size * (entry + which // 2)

    def add(row, y):
        out[:, row] += y

    batches(plan, start, entry, plan[which], packed, blocks, add)
    if when == "far":
        now[...] = out[0]


def past_field(when, steps, plan, blocks, parts, base=None, slots=None):
    places, group_blocks, columns, width = parts[0].shape
    shape = (group_blocks, columns, width)
    packed = VMEM((len(parts) * places * group_blocks + 1, 2 * columns, width), BF16)
    out = [jax.ShapeDtypeStruct((steps - (when == "late"),) + shape, F32)]
    if when == "far":
        out.append(jax.ShapeDtypeStruct(shape, F32))
    scalars = [plan] + [slots] * (when == "late")
    given = [blocks] + [base] * (when != "near")
    return pl.pallas_call(
        functools.partial(past_kernel, when),
        in_specs=[whole(SMEM)] * len(scalars) + [whole(VMEM)] * (len(given) + len(parts)),
        out_specs=[whole(VMEM)] * len(out),
        out_shape=out,
        scratch_shapes=[packed],
        compiler_params=pltpu.CompilerParams(vmem_limit_bytes=16 << 20),
        cost_estimate=BRIEF,
        name=when + "_field",
    )(*scalars, *given, *parts)


def solve(inverse, right, out):
    for i in range(out.shape[0]):
        high, low = halves(right[i])
        y = times(jnp.concatenate([high, low], axis=0), inverse[i]).reshape((2,) + out.shape[1:])
        out[i] = y[0] + y[1]


def summed(refs, t):
    total = refs[0][t]
    for r in refs[1:]:
        total = total + r[t]
    return total


def first_kernel(inverse, incident, *refs):
    *terms, out, right = refs
    right[...] = incident[0] - summed(terms, ...)
    solve(inverse, right, out)


def first_currents(inverse, incident, terms):
    shape = incident.shape[1:]
    return pl.pallas_call(
        first_kernel,
        in_specs=[whole(VMEM)] * (2 + len(terms)),
        out_specs=whole(VMEM),
        out_shape=jax.ShapeDtypeStruct(shape, F32),
        scratch_shapes=[VMEM(shape, F32)],
        compiler_params=pltpu.CompilerParams(vmem_limit_bytes=16 << 20),
        cost_estimate=BRIEF,
        name="first_currents",
    )(inverse, incident, *terms)


def recent(kind, plan, places, packed, blocks, add):
    start = places + kind * room(blocks.shape[0]) * 3
    batches(plan, start, 3, plan[kind], packed, blocks, lambda row, y: add(row, y[0]))


def right_side(rights, t):
    if len(rights) == 1:
        return rights[0][t]
    return rights[0][t + 1] - summed(rights[1:], t)


def step_kernel(places, count, done, plan, blocks, inverse, *refs):
    rights, refs = refs[:count], refs[count:]
    earlier, parts, (out, packed, right) = refs[:done], refs[done:-3], refs[-3:]
    group_blocks, columns, width = right.shape
    for k in range(len(parts)):
        pack(packed, k * group_blocks, parts[k][...])
    packed[len(parts) * group_blocks] = jnp.zeros((2 * columns, width), BF16)
    right[...] = right_side(rights, 0)

    def add(row, y):
        right[row] -= y

    recent(0, plan, places, packed, blocks, add)
    if done:
        last = out.shape[0] - 1
        out[:last] = earlier[0][...]
        out = out.at[last]
    solve(inverse, right, out)


def next_currents(places, plan, blocks, inverse, rights, parts, earlier=None):
    shape = parts[0].shape
    packed = (len(parts) * shape[0] + 1, 2 * shape[1], shape[2])
    scratch = [VMEM(shape, F32)]
    if earlier is None:
        given, out = [], [jax.ShapeDtypeStruct(shape, F32), jax.ShapeDtypeStruct(packed, BF16)]
    else:
        given, out = [earlier], [jax.ShapeDtypeStruct((earlier.shape[0] + 1,) + shape, F32)]
        scratch.insert(0, VMEM(packed, BF16))
    return pl.pallas_call(
        functools.partial(step_kernel, places, len(rights), len(given)),
        in_specs=[whole(SMEM)] + [whole(VMEM)] * (2 + len(rights) + len(given) + len(parts)),
        out_specs=[whole(VMEM)] * len(out),
        out_shape=out,
        scratch_shapes=scratch,
        compiler_params=pltpu.CompilerParams(vmem_limit_bytes=16 << 20),
        cost_estimate=BRIEF,
        name="next_currents",
    )(plan, blocks, inverse, *rights, *given, *parts)


def older_kernel(places, count, plan, blocks, packed, newest, *refs):
    rights, earlier, (out, stacked) = refs[:count], refs[count:-2], refs[-2:]
    if earlier:
        stacked[: stacked.shape[0] - 1] = earlier[0][...]
    stacked[stacked.shape[0] - 1] = newest[...]
    for t in range(out.shape[0]):
        out[t] = right_side(rights, t + 1)

        def add(row, y):
            out[t, row] -= y

        recent(t + 1, plan, places, packed, blocks, add)


def older_field(places, steps, plan, blocks, packed, newest, rights, earlier):
    given = [] if earlier is None else [earlier]
    stacked = (sum(x.shape[0] for x in given) + 1,) + newest.shape
    return pl.pallas_call(
        functools.partial(older_kernel, places, len(rights)),
        in_specs=[whole(SMEM)] + [whole(VMEM)] * (3 + len(rights) + len(given)),
        out_specs=[whole(VMEM)] * 2,
        out_shape=[jax.ShapeDtypeStruct((steps,) + newest.shape, F32), jax.ShapeDtypeStruct(stacked, F32)],
        compiler_params=pltpu.CompilerParams(vmem_limit_bytes=16 << 20),
        cost_estimate=BRIEF,
        name="older_field",
    )(plan, blocks, packed, newest, *rights, *given)


def summands(x):
    bands = lax.axis_size("delay")
    if bands <= 8:
        return [x] + [swap(x, "delay", k) for k in range(2, bands, 2)]
    return [doubled(x)]


def front_summands(x):
    bands = lax.axis_size("delay")
    if bands > 8:
        return [doubled(x)]
    terms = [x]
    for c in range(bands - 2, 0, -2):
        goes = {i: i ^ 1 for i in range(bands)} | {c: 0, 0: 1, 1: c + 1, c + 1: c}
        terms.append(lax.ppermute(x, "delay", list(goes.items())))
    return terms


def doubled(x):
    bit = 2
    while bit < lax.axis_size("delay"):
        x = x + swap(x, "delay", bit)
        bit *= 2
    return x


def from_front(x):
    bands = lax.axis_size("delay")
    mine = lax.axis_index("delay")
    bit = bands // 2
    while bit > 1:
        goes = {i: i ^ 1 for i in range(bands)}
        for i in range(0, bands, 2 * bit):
            goes |= {i: i + bit, i + bit: i + bit + 1, i + bit + 1: i + 1, i + 1: i}
        other = lax.ppermute(x, "delay", list(goes.items()))
        x = jnp.where((mine & (2 * bit - 1)) == bit, other, x)
        bit //= 2
    return x


AT_ONCE = {2: ((0, 2, 3), (1, 5), (4, 6, 7)), 4: ((0, 4, 5), (1, 7), (2, 3, 6)), 6: ((0, 6, 7, 1), (2, 3), (4, 5))}


def from_front_at_once(x):
    if lax.axis_size("delay") != 8:
        return from_front(x)
    pair = lax.axis_index("delay") // 2 * 2
    y = x
    for c, cycles in reversed(AT_ONCE.items()):
        goes = [(a, b) for cycle in cycles for a, b in zip(cycle, cycle[1:] + cycle[:1])]
        y = jnp.where(pair == c, lax.ppermute(x, "delay", goes), y)
    return y


def from_even(x):
    return jnp.where((lax.axis_index("delay") & 1) != 0, swap(x, "delay", 1), x)


def body(history, slot_map, interaction, pattern, live, near_inverse, incident):
    slot_count = history.shape[0]
    moments = incident.shape[0]
    groups = lax.axis_size("src")
    bands = lax.axis_size("delay")
    assert 1 < moments <= slot_count + 1
    assert groups & (groups - 1) == 0 and bands & (bands - 1) == 0
    me = lax.axis_index("src").reshape(1)
    band = lax.axis_index("delay").reshape(1)

    def front_over_src(x):
        pairs = [[(i * bands + j, (i ^ k) * bands if j == 0 else i * bands + j % (bands - 1) + 1)
                  for i in range(groups) for j in range(bands)] for k in range(1, groups)]
        return [x] + [lax.ppermute(x, ("src", "delay"), p) for p in pairs]

    parts = [history] + [swap(history, "src", k) for k in range(1, groups)]
    ring = [(i, (i + 1) % bands) for i in range(bands)]
    slots_before = lax.ppermute(slot_map, "delay", ring)
    blocks, inverse = split_blocks(interaction, near_inverse)
    past, newer = make_plan(groups, history.shape[1], moments, me, band, pattern, live, slot_map)
    parts[1], slots_before, past, newer, blocks, inverse = lax.optimization_barrier(
        (parts[1], slots_before, past, newer, blocks, inverse)
    )
    (field,) = past_field("near", moments, past, blocks, parts[:2])
    field, parts[2:] = lax.optimization_barrier((field, parts[2:]))
    before = [lax.ppermute(p, "delay", ring) for p in parts]
    field, now = past_field("far", moments, past, blocks, parts[2:], field)
    now = now + swap(now, "delay", 1)
    now, field = lax.optimization_barrier((now, field))
    (later,) = past_field("late", moments, past, blocks, before, field, slots_before)
    first = newest = first_currents(inverse, incident, summands(now))
    earlier = None
    for moment in range(1, moments):
        shared = front_over_src(newest)
        if moment == 1:
            rights = [incident] + front_summands(later + swap(later, "delay", 1))
        else:
            rights, earlier = older_field(
                slot_count, moments - moment, newer, blocks, packed, newest, rights, earlier
            )
            rights = [rights]
        made = next_currents(
            slot_count, newer, blocks, inverse, rights, shared, earlier if moment > 1 and moment + 1 == moments else None
        )
        if len(made) > 1:
            newest, packed = made
    (others,) = made if len(made) == 1 else (newest[None],)
    return jnp.concatenate([first[None], from_even(from_front_at_once(others))])


def solution(mesh):
    return jax.shard_map(
        body,
        mesh=mesh,
        in_specs=(
            P("delay", "src", None, None),
            P("delay"),
            P(("src", "delay"), None, None),
            P(None, ("src", "delay")),
            P(("src", "delay")),
            P("src", None, None),
            P(None, "src", None, None),
        ),
        out_specs=P(None, "src", None, None),
        check_vma=False,
    )
```

```python
import functools

import jax
import jax.numpy as jnp
from jax import lax
from jax.experimental import pallas as pl
from jax.experimental.pallas import tpu as pltpu
from jax.sharding import PartitionSpec as P

F32 = jnp.float32
BF16 = jnp.bfloat16
VMEM = pltpu.VMEM
SMEM = pltpu.SMEM
UNROLL = 16
BRIEF = pl.CostEstimate(flops=1, bytes_accessed=1, transcendentals=0)


def whole(space):
    return pl.BlockSpec(memory_space=space)


def swap(x, axis, bits):
    n = lax.axis_size(axis)
    return lax.ppermute(x, axis, [(i, i ^ bits) for i in range(n)])


def halves(x):
    high = x.astype(BF16)
    low = (x - high.astype(F32)).astype(BF16)
    return high, low


def wide(x):
    high, low = halves(x)
    return jnp.concatenate([high, low], axis=-1)


def times(rows, weights):
    both = jnp.concatenate([rows, rows], axis=-1)
    return lax.dot_general(both, weights, (((1,), (1,)), ((), ())), preferred_element_type=F32)


def room(pairs):
    return (pairs + UNROLL - 1) // UNROLL * UNROLL + UNROLL


def plan_kernel(groups, group_blocks, steps, me, band, pattern, live, slots, near, far, late, later, newest, older, held, count):
    places = slots.shape[0]
    size = room(pattern.shape[1])
    cells = places * group_blocks
    for d in range(places):
        held[d] = sum(jnp.where(slots[j] == d, j, 0) for j in range(places))
        count[d] = 0

    def put(ref, to, e, row, cell):
        ref[to] = e
        ref[to + 1] = row
        for t in range(len(cell)):
            ref[to + 2 + t] = cell[t]

    def put_newer(d, n, e, row, cell):
        @pl.when(d == 0)
        def _():
            put(newest, 1 + n * 3, e, row, [cell])

        @pl.when(d != 0)
        def _():
            put(older, places - 1 + ((d - 1) * size + n) * 3, e, row, [cell])

    def place(e, taken):
        n_near, n_far, n_late, n_later = taken
        row, column, d = pattern[0, e], pattern[1, e], pattern[2, e]
        group = (column // group_blocks) ^ me[0]
        block = column % group_blocks
        is_far = (group >= 2).astype(jnp.int32)
        nothing = jnp.where(is_far == 1, (groups - 2) * cells, 2 * cells)
        cell = [
            jnp.where(
                d >= t, ((group - 2 * is_far) * places + held[jnp.maximum(d - t, 0)]) * group_blocks + block, nothing
            )
            for t in range(steps)
        ]

        @pl.when(is_far == 0)
        def _():
            put(near, 1 + n_near * (2 + steps), e, row, cell)

        @pl.when(is_far == 1)
        def _():
            put(far, 1 + n_far * (2 + steps), e, row, cell)

        before = [
            jnp.where(d < t, ((group - 2 * is_far) * places + d - t + places) * group_blocks + block, nothing)
            for t in range(1, steps)
        ]

        @pl.when(is_far == 0)
        def _():
            put(late, 1 + n_late * (1 + steps), e, row, before)

        @pl.when(is_far == 1)
        def _():
            put(later, 1 + n_later * (1 + steps), e, row, before)

        n = count[d]
        count[d] = n + 1
        put_newer(d, n, e, row, group * group_blocks + block)
        reads = (d < steps - 1).astype(jnp.int32)
        return n_near + 1 - is_far, n_far + is_far, n_late + reads * (1 - is_far), n_later + reads * is_far

    zero = jnp.int32(0)
    n_near, n_far, n_late, n_later = lax.fori_loop(0, live[0], place, (zero, zero, zero, zero))
    near[0] = n_near
    far[0] = n_far
    late[0] = jnp.where(band[0] == 0, 0, n_late)
    later[0] = jnp.where(band[0] == 0, 0, n_later)

    def fill(i, c):
        put(near, 1 + (n_near + i) * (2 + steps), 0, 0, [2 * cells] * steps)
        put(far, 1 + (n_far + i) * (2 + steps), 0, 0, [(groups - 2) * cells] * steps)
        put(late, 1 + (n_late + i) * (1 + steps), 0, 0, [2 * cells] * (steps - 1))
        put(later, 1 + (n_later + i) * (1 + steps), 0, 0, [(groups - 2) * cells] * (steps - 1))
        put(newest, 1 + (count[0] + i) * 3, 0, 0, [groups * group_blocks])
        for d in range(1, places):
            put(older, places - 1 + ((d - 1) * size + count[d] + i) * 3, 0, 0, [groups * group_blocks])
        return c

    lax.fori_loop(0, UNROLL, fill, 0)
    newest[0] = jnp.where(band[0] == 0, count[0], 0)
    for d in range(1, places):
        older[d - 1] = jnp.where(band[0] == 0, count[d], 0)


def make_plan(groups, group_blocks, steps, me, band, pattern, live, slots):
    places = slots.shape[0]
    size = room(pattern.shape[1])
    lengths = [1 + size * (2 + steps)] * 2 + [1 + size * (1 + steps)] * 2 + [1 + size * 3, (places - 1) * (1 + size * 3)]
    return pl.pallas_call(
        functools.partial(plan_kernel, groups, group_blocks, steps),
        in_specs=[whole(SMEM)] * 5,
        out_specs=[whole(SMEM)] * len(lengths),
        out_shape=[jax.ShapeDtypeStruct((n,), jnp.int32) for n in lengths],
        scratch_shapes=[SMEM((places,), jnp.int32), SMEM((places,), jnp.int32)],
        name="make_plan",
    )(me, band, pattern, live, slots)


def split_kernel(blocks, inverse, wide_blocks, wide_inverse, held, held_inverse, sems):
    chunks = sems.shape[0] - 1
    per = blocks.shape[0] // chunks
    copies = [
        pltpu.make_async_copy(blocks.at[pl.ds(k * per, per)], held.at[pl.ds(k * per, per)], sems.at[k])
        for k in range(chunks)
    ]
    copies.append(pltpu.make_async_copy(inverse, held_inverse, sems.at[chunks]))
    for c in copies:
        c.start()
    for k in range(chunks):
        copies[k].wait()

        def split(e, c):
            wide_blocks[e] = wide(held[e])
            return c

        lax.fori_loop(k * per, (k + 1) * per, split, 0, unroll=4)
    copies[chunks].wait()
    wide_inverse[...] = wide(held_inverse[...])


def split_blocks(blocks, inverse):
    pairs, a, q = blocks.shape
    chunks = 4 if pairs % 4 == 0 else 1
    return pl.pallas_call(
        split_kernel,
        in_specs=[whole(pltpu.HBM)] * 2,
        out_specs=[whole(VMEM)] * 2,
        out_shape=[
            jax.ShapeDtypeStruct((pairs, a, 2 * q), BF16),
            jax.ShapeDtypeStruct((inverse.shape[0], a, 2 * q), BF16),
        ],
        scratch_shapes=[VMEM(blocks.shape, F32), VMEM(inverse.shape, F32), pltpu.SemaphoreType.DMA((chunks + 1,))],
        compiler_params=pltpu.CompilerParams(vmem_limit_bytes=16 << 20),
        cost_estimate=pl.CostEstimate(flops=8 * pairs * a * q, bytes_accessed=8 * pairs * a * q, transcendentals=0),
        name="split_blocks",
    )(blocks, inverse)


def pack(packed, start, x):
    high, low = halves(x)
    packed[pl.ds(start, x.shape[0])] = jnp.concatenate([high, low], axis=1)


def batches(plan, start, entry, amount, packed, blocks, add):
    def batch(i, carry):
        made = []
        for u in range(UNROLL):
            at = start + (i * UNROLL + u) * entry
            rows = [packed[plan[at + 2 + t]] for t in range(entry - 2)]
            made.append((plan[at + 1], times(jnp.concatenate(rows, axis=0), blocks[plan[at]])))
        for row, y in made:
            y = y.reshape(entry - 2, 2, packed.shape[1] // 2, y.shape[-1])
            add(row, y[:, 0] + y[:, 1])
        return carry

    lax.fori_loop(0, (amount + UNROLL - 1) // UNROLL, batch, 0)


def past_kernel(when, plan, *refs):
    if when == "near":
        blocks, *parts, out, packed = refs
        out[...] = jnp.zeros_like(out)
    elif when == "far":
        blocks, base, *parts, out, now, packed = refs
        out[...] = base[...]
    else:
        slots, blocks, base, *parts, out, packed = refs
        out[...] = base[1:] if when == "late" else base[...]
    places, group_blocks, columns, width = parts[0].shape
    cells = places * group_blocks
    for k in range(len(parts)):
        if when in ("late", "later"):
            for j in range(places):
                pack(packed, (k * places + slots[j]) * group_blocks, parts[k][j])
        else:
            pack(packed, k * cells, parts[k][...].reshape(cells, columns, width))
    packed[len(parts) * cells] = jnp.zeros((2 * columns, width), BF16)

    def add(row, y):
        out[:, row] += y

    batches(plan, 1, 2 + out.shape[0], plan[0], packed, blocks, add)
    if when == "far":
        now[...] = out[0]


def past_field(when, steps, plan, blocks, parts, base=None, slots=None):
    places, group_blocks, columns, width = parts[0].shape
    shape = (group_blocks, columns, width)
    packed = VMEM((len(parts) * places * group_blocks + 1, 2 * columns, width), BF16)
    out = [jax.ShapeDtypeStruct((steps - (when in ("late", "later")),) + shape, F32)]
    if when == "far":
        out.append(jax.ShapeDtypeStruct(shape, F32))
    scalars = [plan] + [slots] * (when in ("late", "later"))
    given = [blocks] + [base] * (when != "near")
    return pl.pallas_call(
        functools.partial(past_kernel, when),
        in_specs=[whole(SMEM)] * len(scalars) + [whole(VMEM)] * (len(given) + len(parts)),
        out_specs=[whole(VMEM)] * len(out),
        out_shape=out,
        scratch_shapes=[packed],
        compiler_params=pltpu.CompilerParams(vmem_limit_bytes=16 << 20),
        cost_estimate=BRIEF,
        name=when + "_field",
    )(*scalars, *given, *parts)


def solve(inverse, right, out):
    for i in range(out.shape[0]):
        high, low = halves(right[i])
        y = times(jnp.concatenate([high, low], axis=0), inverse[i]).reshape((2,) + out.shape[1:])
        out[i] = y[0] + y[1]


def summed(refs, t):
    total = refs[0][t]
    for r in refs[1:]:
        total = total + r[t]
    return total


def first_kernel(inverse, incident, *refs):
    *terms, out, right = refs
    right[...] = incident[0] - summed(terms, ...)
    solve(inverse, right, out)


def first_currents(inverse, incident, terms):
    shape = incident.shape[1:]
    return pl.pallas_call(
        first_kernel,
        in_specs=[whole(VMEM)] * (2 + len(terms)),
        out_specs=whole(VMEM),
        out_shape=jax.ShapeDtypeStruct(shape, F32),
        scratch_shapes=[VMEM(shape, F32)],
        compiler_params=pltpu.CompilerParams(vmem_limit_bytes=16 << 20),
        cost_estimate=BRIEF,
        name="first_currents",
    )(inverse, incident, *terms)


def right_side(rights, t):
    if len(rights) == 1:
        return rights[0][t]
    return rights[0][t + 1] - summed(rights[1:], t)


def step_kernel(count, done, plan, blocks, inverse, *refs):
    rights, refs = refs[:count], refs[count:]
    earlier, parts, (out, packed, right) = refs[:done], refs[done:-3], refs[-3:]
    group_blocks, columns, width = right.shape
    for k in range(len(parts)):
        pack(packed, k * group_blocks, parts[k][...])
    packed[len(parts) * group_blocks] = jnp.zeros((2 * columns, width), BF16)
    right[...] = right_side(rights, 0)

    def add(row, y):
        right[row] -= y

    batches(plan, 1, 3, plan[0], packed, blocks, lambda row, y: add(row, y[0]))
    if done:
        last = out.shape[0] - 1
        out[:last] = earlier[0][...]
        out = out.at[last]
    solve(inverse, right, out)


def next_currents(plan, blocks, inverse, rights, parts, earlier=None):
    shape = parts[0].shape
    packed = (len(parts) * shape[0] + 1, 2 * shape[1], shape[2])
    scratch = [VMEM(shape, F32)]
    if earlier is None:
        given, out = [], [jax.ShapeDtypeStruct(shape, F32), jax.ShapeDtypeStruct(packed, BF16)]
    else:
        given, out = [earlier], [jax.ShapeDtypeStruct((earlier.shape[0] + 1,) + shape, F32)]
        scratch.insert(0, VMEM(packed, BF16))
    return pl.pallas_call(
        functools.partial(step_kernel, len(rights), len(given)),
        in_specs=[whole(SMEM)] + [whole(VMEM)] * (2 + len(rights) + len(given) + len(parts)),
        out_specs=[whole(VMEM)] * len(out),
        out_shape=out,
        scratch_shapes=scratch,
        compiler_params=pltpu.CompilerParams(vmem_limit_bytes=16 << 20),
        cost_estimate=BRIEF,
        name="next_currents",
    )(plan, blocks, inverse, *rights, *given, *parts)


def older_kernel(places, count, plan, blocks, packed, newest, *refs):
    rights, earlier, (out, stacked) = refs[:count], refs[count:-2], refs[-2:]
    if earlier:
        stacked[: stacked.shape[0] - 1] = earlier[0][...]
    stacked[stacked.shape[0] - 1] = newest[...]
    for t in range(out.shape[0]):
        out[t] = right_side(rights, t + 1)

        def add(row, y):
            out[t, row] -= y

        start = places - 1 + t * room(blocks.shape[0]) * 3
        batches(plan, start, 3, plan[t], packed, blocks, lambda row, y: add(row, y[0]))


def older_field(places, steps, plan, blocks, packed, newest, rights, earlier):
    given = [] if earlier is None else [earlier]
    stacked = (sum(x.shape[0] for x in given) + 1,) + newest.shape
    return pl.pallas_call(
        functools.partial(older_kernel, places, len(rights)),
        in_specs=[whole(SMEM)] + [whole(VMEM)] * (3 + len(rights) + len(given)),
        out_specs=[whole(VMEM)] * 2,
        out_shape=[jax.ShapeDtypeStruct((steps,) + newest.shape, F32), jax.ShapeDtypeStruct(stacked, F32)],
        compiler_params=pltpu.CompilerParams(vmem_limit_bytes=16 << 20),
        cost_estimate=BRIEF,
        name="older_field",
    )(plan, blocks, packed, newest, *rights, *given)


def summands(x):
    bands = lax.axis_size("delay")
    if bands <= 8:
        return [x] + [swap(x, "delay", k) for k in range(bands - 2, 0, -2)]
    return [doubled(x)]


def front_summands(x):
    bands = lax.axis_size("delay")
    if bands > 8:
        return [doubled(x)]
    terms = [x]
    for c in range(bands - 2, 0, -2):
        goes = {i: i ^ 1 for i in range(bands)} | {c: 0, 0: 1, 1: c + 1, c + 1: c}
        terms.append(lax.ppermute(x, "delay", list(goes.items())))
    return terms


def doubled(x):
    bit = 2
    while bit < lax.axis_size("delay"):
        x = x + swap(x, "delay", bit)
        bit *= 2
    return x


def from_front(x):
    bands = lax.axis_size("delay")
    mine = lax.axis_index("delay")
    bit = bands // 2
    while bit > 1:
        goes = {i: i ^ 1 for i in range(bands)}
        for i in range(0, bands, 2 * bit):
            goes |= {i: i + bit, i + bit: i + bit + 1, i + bit + 1: i + 1, i + 1: i}
        other = lax.ppermute(x, "delay", list(goes.items()))
        x = jnp.where((mine & (2 * bit - 1)) == bit, other, x)
        bit //= 2
    return x


AT_ONCE = {2: ((0, 2, 3), (1, 5), (4, 6, 7)), 4: ((0, 4, 5), (1, 7), (2, 3, 6)), 6: ((0, 6, 7, 1), (2, 3), (4, 5))}


def from_front_at_once(x):
    if lax.axis_size("delay") != 8:
        return from_front(x)
    pair = lax.axis_index("delay") // 2 * 2
    y = x
    for c, cycles in reversed(AT_ONCE.items()):
        goes = [(a, b) for cycle in cycles for a, b in zip(cycle, cycle[1:] + cycle[:1])]
        y = jnp.where(pair == c, lax.ppermute(x, "delay", goes), y)
    return y


def from_even(x):
    return jnp.where((lax.axis_index("delay") & 1) != 0, swap(x, "delay", 1), x)


def body(history, slot_map, interaction, pattern, live, near_inverse, incident):
    slot_count = history.shape[0]
    moments = incident.shape[0]
    groups = lax.axis_size("src")
    bands = lax.axis_size("delay")
    assert 1 < moments <= slot_count + 1
    assert groups & (groups - 1) == 0 and bands & (bands - 1) == 0
    me = lax.axis_index("src").reshape(1)
    band = lax.axis_index("delay").reshape(1)

    def front_over_src(x):
        pairs = [[(i * bands + j, (i ^ k) * bands if j == 0 else i * bands + j % (bands - 1) + 1)
                  for i in range(groups) for j in range(bands)] for k in range(1, groups)]
        return [x] + [lax.ppermute(x, ("src", "delay"), p) for p in pairs]

    parts = [history] + [swap(history, "src", k) for k in range(1, groups)]
    ring = [(i, (i + 1) % bands) for i in range(bands)]
    slots_before = lax.ppermute(slot_map, "delay", ring)
    blocks, inverse = split_blocks(interaction, near_inverse)
    plan = make_plan(groups, history.shape[1], moments, me, band, pattern, live, slot_map)
    parts[1], slots_before, plan, blocks, inverse = lax.optimization_barrier(
        (parts[1], slots_before, plan, blocks, inverse)
    )
    near_list, far_list, late_list, later_list, newest_list, older_list = plan
    (field,) = past_field("near", moments, near_list, blocks, parts[:2])
    field, parts[2:] = lax.optimization_barrier((field, parts[2:]))
    before = [lax.ppermute(p, "delay", ring) for p in parts]
    field, now = past_field("far", moments, far_list, blocks, parts[2:], field)
    now = now + swap(now, "delay", 1)
    now, field = lax.optimization_barrier((now, field))
    (later,) = past_field("late", moments, late_list, blocks, before[:2], field, slots_before)
    (later,) = past_field("later", moments, later_list, blocks, before[2:], later, slots_before)
    first = newest = first_currents(inverse, incident, summands(now))
    earlier = None
    for moment in range(1, moments):
        shared = front_over_src(newest)
        if moment == 1:
            rights = [incident] + front_summands(later + swap(later, "delay", 1))
        else:
            rights, earlier = older_field(
                slot_count, moments - moment, older_list, blocks, packed, newest, rights, earlier
            )
            rights = [rights]
        made = next_currents(
            newest_list, blocks, inverse, rights, shared, earlier if moment > 1 and moment + 1 == moments else None
        )
        if len(made) > 1:
            newest, packed = made
    (others,) = made if len(made) == 1 else (newest[None],)
    return jnp.concatenate([first[None], from_even(from_front_at_once(others))])


def solution(mesh):
    return jax.shard_map(
        body,
        mesh=mesh,
        in_specs=(
            P("delay", "src", None, None),
            P("delay"),
            P(("src", "delay"), None, None),
            P(None, ("src", "delay")),
            P(("src", "delay")),
            P("src", None, None),
            P(None, "src", None, None),
        ),
        out_specs=P(None, "src", None, None),
        check_vma=False,
    )
```
